128 devices in a mesh: row: 16 (over x, z), col: 8 (over y, core).
Axes of the slice: x: 4, y: 4, z: 4, core: 2. Of those that a mesh axis runs over, the one named last changes fastest.
Arguments:
- posteriors: bfloat16 [8192, 256, 256], P(('row', 'col'))
- pair_anchor: int32 [8192], P(('row', 'col')), may hold values from 0 to 15, as said below
- pair_column: int32 [8192], P(('row', 'col')), may hold values from 0 to 511
- inter: int32 [32, 4], replicated, may hold values from 0 to 15, all different within a row
- lengths: int32 [512], replicated, may hold values from 32 to 256
Outputs:
- consistent: bfloat16 [32, 512, 256, 256], P(None, ('row', 'col'))
The draws below stay inside these ranges and needn't reach their ends.
Inputs may be any that keep to these rules, and one draw needn't show every extreme that they name: `pair_anchor`: each anchor and family sequence pair (a, y) stands in exactly one slot over all devices. The slots of one device hold at most 1 pairs whose columns lie in one aligned block of 4 columns, and every device reaches that bound for some block. `inter`: the 4 anchors of a row differ.
All inputs are finite; a program needn't handle non-finite values.
Results may differ from the reference program's by a relative error of at most 0.001.
Values may be sent and summed in bfloat16 or wider, within the bound.
No kernel may reach another device: no remote copies, remote signals or barrier semaphores. Data moves between devices by JAX's collectives and lax.ppermute only.
A program may use at most 384 MiB of HBM per device.

```python
import jax
import jax.numpy as jnp
from jax import lax

L = 256
NZ = 16
INTER = 4
YB = 4
X = 32
NSEQ = 512
SLOTS = 64
CAP = 1
PAIRS = 8192
DEVICES = 128


def pair_layout(key):
    base_key = jax.random.fold_in(key, 911)
    half_slots = SLOTS // 2
    half_size = max(1, CAP // 2)
    spread = jax.random.permutation(jax.random.fold_in(base_key, 1), DEVICES).astype(jnp.int32)
    groups_of = jax.random.permutation(jax.random.fold_in(base_key, 2), SLOTS).astype(jnp.int32)
    group_of = jnp.where(groups_of < half_slots, groups_of // CAP, half_slots // CAP + (groups_of - half_slots) // half_size)
    offset = spread[group_of]
    scores = jax.random.randint(jax.random.fold_in(base_key, 3), (DEVICES, SLOTS), 0, 1 << 20) * SLOTS
    scores = scores + jnp.arange(SLOTS, dtype=jnp.int32)[None, :]
    within = jnp.argsort(scores, axis=1).astype(jnp.int32)
    source = jnp.arange(DEVICES, dtype=jnp.int32)[:, None]
    target = (source - offset[within]) % DEVICES
    anchor = within // YB
    column = target * YB + within % YB
    return (anchor.reshape(-1).astype(jnp.int32), column.reshape(-1).astype(jnp.int32))


def draw_pair_anchor(key, part):
    return pair_layout(key)[0]


def draw_pair_column(key, part):
    return pair_layout(key)[1]


def draw_posteriors(key, part):
    uniform_part = jax.random.uniform(jax.random.fold_in(key, 5), (PAIRS, L, L), jnp.float32)
    return (2.0 / jnp.sqrt(L * 1.0) * uniform_part).astype(jnp.bfloat16)


def plant(result, rng, smallest, high):
    longest = result.shape.index(max(result.shape))
    spots = []
    for shift in (0, 1):
        where = [jax.random.randint(jax.random.fold_in(rng, axis), (), 0, length) for axis, length in enumerate(result.shape)]
        where[longest] = (where[longest] + shift) % result.shape[longest]
        spots.append(tuple(where))
    return result.at[spots[0]].set(smallest).at[spots[1]].set(high)


def distinct(rng, rows, amount, top, lift):
    order = jax.random.permutation(jax.random.fold_in(rng, 1), amount)
    boost = order
    for power in range(3):
        boost = boost * boost // amount
    boost = boost * lift // amount
    chance = jax.random.randint(jax.random.fold_in(rng, 2), (rows, amount), 0, 4096) + boost
    fixed_rows = jax.random.permutation(jax.random.fold_in(rng, 3), rows)[jnp.arange(amount) % rows]
    chance = jnp.where(jnp.arange(rows)[:, None] == fixed_rows[None, :], 1 << 14, chance)
    merit = chance * amount + jnp.arange(amount)
    return lax.top_k(merit.astype(jnp.int32), top)[1].astype(jnp.int32)


def setup_inputs(seed: int = 0) -> dict:
    arg_keys = jax.random.split(jax.random.key(seed), 6)
    return {
        "posteriors": draw_posteriors(jax.random.fold_in(arg_keys[5], 71), 0),
        "pair_anchor": draw_pair_anchor(jax.random.fold_in(arg_keys[5], 71), 0),
        "pair_column": draw_pair_column(jax.random.fold_in(arg_keys[5], 71), 0),
        "inter": distinct(arg_keys[3], X, NZ, INTER, 0),
        "lengths": plant(jax.random.randint(arg_keys[4], (NSEQ,), L // 8, L + 1), jax.random.fold_in(arg_keys[4], 1), L // 8, L).astype(jnp.int32),
    }


def reference(posteriors, pair_anchor, pair_column, inter, lengths):
    place = (pair_anchor * NSEQ + pair_column).astype(jnp.int32)
    slab = jnp.zeros((NZ * NSEQ, L, L), jnp.bfloat16).at[place].set(posteriors)
    slab = slab.reshape(NZ, NSEQ, L, L)
    position = jnp.arange(L, dtype=jnp.int32)
    col_mask = (position[None, :] < lengths[:, None]).astype(jnp.float32)

    def one_row(row_index):
        chosen = inter[row_index]
        summed = jnp.zeros((NSEQ, L, L), jnp.float32)
        for term in range(INTER):
            left_side = slab[chosen[term], row_index].astype(jnp.float32)
            right_side = slab[chosen[term]].astype(jnp.float32)
            summed = summed + jnp.einsum("mi,ymj->yij", left_side, right_side)
        row_mask = (position < lengths[row_index]).astype(jnp.float32)
        scaled = summed * (1.0 / INTER) * row_mask[None, :, None] * col_mask[:, None, :]
        return scaled.astype(jnp.bfloat16)

    return lax.map(one_row, jnp.arange(X, dtype=jnp.int32))
```

```python
import jax
import jax.numpy as jnp
from jax import lax
from jax.experimental import pallas as pl
from jax.experimental.pallas import tpu as pltpu
from jax.sharding import PartitionSpec as P

NZ = 16
INTER = 4
YB = 4
STORES = 4
AXES = ("row", "col")
VMEM_LIMIT = 56 * 1024 * 1024
TRANSFORM_VMEM = 56 * 1024 * 1024


def pack_kernel(slot_target_ref, blocks_ref, out_ref, held_ref, load_sems, store_sem):
    chunks = load_sems.shape[0]
    slots = held_ref.shape[0]
    chunk = slots // chunks

    def load(c):
        part = pl.ds(c * chunk, chunk)
        return pltpu.make_async_copy(blocks_ref.at[part], held_ref.at[part], load_sems.at[c])

    for c in range(chunks):
        load(c).start()
    for c in range(chunks):
        load(c).wait()
        for s in range(c * chunk, (c + 1) * chunk):
            pltpu.make_async_copy(
                held_ref.at[s], out_ref.at[slot_target_ref[s]], store_sem
            ).start()
    pltpu.make_async_copy(held_ref, out_ref.at[pl.ds(0, slots)], store_sem).wait()


def pack(posteriors, slot_target, devices):
    slots, side, _ = posteriors.shape
    chunks = 8
    return pl.pallas_call(
        pack_kernel,
        out_shape=jax.ShapeDtypeStruct((devices, side, side), posteriors.dtype),
        in_specs=[
            pl.BlockSpec(memory_space=pltpu.SMEM),
            pl.BlockSpec(memory_space=pl.ANY),
        ],
        out_specs=pl.BlockSpec(memory_space=pl.ANY),
        scratch_shapes=[
            pltpu.VMEM((slots, side, side), posteriors.dtype),
            pltpu.SemaphoreType.DMA((chunks,)),
            pltpu.SemaphoreType.DMA,
        ],
        compiler_params=pltpu.CompilerParams(vmem_limit_bytes=VMEM_LIMIT),
        name="pack",
    )(slot_target, posteriors)


def pieces_kernel(owner_slot_ref, sent_key_ref, block_ref, out_ref):
    pieces, _, rows, side = out_ref.shape
    tile = side // pieces
    o = pl.program_id(0)
    owners = pl.num_programs(0)
    turned = block_ref[0].T
    out_ref[:, 0, :tile, :] = turned.reshape(pieces, tile, side)
    for p in range(pieces):
        first = lax.broadcasted_iota(jnp.int32, (rows - tile, side), 0) < (rows - tile) // 2
        keys = jnp.where(first, sent_key_ref[p * owners + o], sent_key_ref[o])
        out_ref[p, 0, tile:, :] = keys.astype(jnp.float32).astype(out_ref.dtype)


def window_pieces(posteriors, owner_slot, sent_key, pieces):
    _, side, _ = posteriors.shape
    owners = owner_slot.shape[0]
    rows = side // pieces + 8
    return pl.pallas_call(
        pieces_kernel,
        out_shape=jax.ShapeDtypeStruct((pieces, owners, rows, side), posteriors.dtype),
        grid_spec=pltpu.PrefetchScalarGridSpec(
            num_scalar_prefetch=2,
            grid=(owners,),
            in_specs=[pl.BlockSpec((1, side, side), lambda o, slot, key: (slot[o], 0, 0))],
            out_specs=pl.BlockSpec((pieces, 1, rows, side), lambda o, slot, key: (0, o, 0, 0)),
        ),
        name="pieces",
    )(owner_slot, sent_key, posteriors)


def pick_kernel(wanted_ref, arrived_ref, picked_ref, source_ref, found_ref, where_ref, sem):
    wanted, tile, side = picked_ref.shape
    devices = arrived_ref.shape[0]
    keys = lax.broadcasted_iota(jnp.int32, (devices, side), 1)
    device = lax.broadcasted_iota(jnp.int32, (devices, side), 0)
    for part in range(2):
        got = arrived_ref[:, tile + 4 * part, :].astype(jnp.float32).astype(jnp.int32)
        found = jnp.sum(jnp.where(got == keys, device, 0), axis=0, keepdims=True)
        found_ref[pl.ds(part, 1), :] = found
    source_ref[...] = found_ref[pl.ds(0, 1), :]
    copy = pltpu.make_async_copy(found_ref, where_ref, sem)
    copy.start()
    copy.wait()
    for q in range(wanted):
        picked_ref[q] = arrived_ref[where_ref[1, wanted_ref[q]], :tile, :]


def pick(arrived, wanted, tile):
    devices, _, side = arrived.shape
    count = wanted.shape[0]
    return pl.pallas_call(
        pick_kernel,
        out_shape=(
            jax.ShapeDtypeStruct((count, tile, side), arrived.dtype),
            jax.ShapeDtypeStruct((1, side), jnp.int32),
        ),
        in_specs=[
            pl.BlockSpec(memory_space=pltpu.SMEM),
            pl.BlockSpec(memory_space=pltpu.VMEM),
        ],
        out_specs=(pl.BlockSpec(memory_space=pltpu.VMEM), pl.BlockSpec(memory_space=pltpu.VMEM)),
        scratch_shapes=[
            pltpu.VMEM((2, side), jnp.int32),
            pltpu.SMEM((2, side), jnp.int32),
            pltpu.SemaphoreType.DMA,
        ],
        name="pick",
    )(wanted, arrived)


def transform_kernel(
    source_ref,
    key_ref,
    row_len_ref,
    col_len_ref,
    window_ref,
    incoming_ref,
    out_ref,
    slab_ref,
    left_ref,
    held_ref,
    slab_sem,
    left_sems,
    out_sems,
):
    keys, side, _ = slab_ref.shape
    count, pieces, _, tile, _ = left_ref.shape
    depth = held_ref.shape[0]

    def fetch_left(g):
        return pltpu.make_async_copy(
            window_ref.at[:, pl.ds(g * INTER, INTER)], left_ref.at[g], left_sems.at[g]
        )

    def store(g, slot):
        return pltpu.make_async_copy(held_ref.at[slot], out_ref.at[g], out_sems.at[slot])

    def fetch(k, carry):
        pltpu.make_async_copy(incoming_ref.at[source_ref[0, k]], slab_ref.at[k], slab_sem).start()
        return carry

    def start_left(g, carry):
        fetch_left(g).start()
        return carry

    lax.fori_loop(0, keys, fetch, 0)
    lax.fori_loop(0, count, start_left, 0)
    pltpu.make_async_copy(incoming_ref.at[pl.ds(0, keys)], slab_ref, slab_sem).wait()

    def one_row(g, carry):
        slot = lax.rem(g, depth)
        row_len = row_len_ref[g]
        fetch_left(g).wait()

        @pl.when(g >= depth)
        def _():
            store(g - depth, slot).wait()

        def compute(height):
            lanes = lax.broadcasted_iota(jnp.int32, (height, side), 1)
            rows = lax.broadcasted_iota(jnp.int32, (height, side), 0)
            lefts = [left_ref[g, : height // tile, k].reshape(height, side) for k in range(INTER)]
            for y in range(YB):
                total = jnp.dot(
                    lefts[0], slab_ref[key_ref[g * INTER] + y], preferred_element_type=jnp.float32
                )
                for k in range(1, INTER):
                    total += jnp.dot(
                        lefts[k],
                        slab_ref[key_ref[g * INTER + k] + y],
                        preferred_element_type=jnp.float32,
                    )
                keep = (rows < row_len) & (lanes < col_len_ref[y])
                held_ref[slot, y, :height, :] = jnp.where(
                    keep, total * (1.0 / INTER), 0.0
                ).astype(held_ref.dtype)

        @pl.when(row_len > side // 2)
        def _():
            compute(side)

        @pl.when(row_len <= side // 2)
        def _():
            compute(side // 2)
            held_ref[slot, :, side // 2 :, :] = jnp.zeros((YB, side // 2, side), held_ref.dtype)

        store(g, slot).start()
        return carry

    lax.fori_loop(0, count, one_row, 0)
    for g in range(count - depth, count):
        store(g, g % depth).wait()


def transform(incoming, window, source, key, row_len, col_len):
    pieces, entries, tile, side = window.shape
    count = entries // INTER
    keys = NZ * YB
    anywhere = pl.BlockSpec(memory_space=pl.ANY)
    return pl.pallas_call(
        transform_kernel,
        out_shape=jax.ShapeDtypeStruct((row_len.shape[0], YB, side, side), incoming.dtype),
        in_specs=[pl.BlockSpec(memory_space=pltpu.SMEM)] * 4 + [anywhere] * 2,
        out_specs=anywhere,
        scratch_shapes=[
            pltpu.VMEM((keys, side, side), incoming.dtype),
            pltpu.VMEM((count, pieces, INTER, tile, side), incoming.dtype),
            pltpu.VMEM((STORES, YB, side, side), incoming.dtype),
            pltpu.SemaphoreType.DMA,
            pltpu.SemaphoreType.DMA((count,)),
            pltpu.SemaphoreType.DMA((STORES,)),
        ],
        cost_estimate=pl.CostEstimate(
            flops=2 * count * YB * INTER * side**3,
            bytes_accessed=2 * (keys + count * (YB + INTER)) * side * side,
            transcendentals=0,
        ),
        compiler_params=pltpu.CompilerParams(vmem_limit_bytes=TRANSFORM_VMEM),
        name="transform",
    )(source, key, row_len, col_len, window, incoming)


def shards(posteriors, pair_anchor, pair_column, inter, lengths):
    devices = lax.axis_size(AXES)
    pieces = lax.axis_size("row")
    owners = lax.axis_size("col")
    me = lax.axis_index(AXES)
    owner = lax.axis_index("col")
    slots, side, _ = posteriors.shape
    x_count = inter.shape[0]
    tile = side // pieces

    slot_target = pair_column // YB
    slot_key = pair_anchor * YB + pair_column % YB
    aims = slot_target[None, :] == jnp.arange(devices, dtype=jnp.int32)[:, None]
    sent_key = slots + jnp.sum(jnp.where(aims, slot_key[None, :] - slots, 0), axis=1)
    slot_ids = jnp.arange(slots, dtype=jnp.int32)
    owner_slot = jnp.sum(jnp.where(aims[:owners], slot_ids[None, :], 0), axis=1)

    cut = window_pieces(posteriors, owner_slot, sent_key, pieces)
    arrived = lax.all_to_all(
        cut.reshape(devices, tile + 8, side), AXES, split_axis=0, concat_axis=0, tiled=True
    )

    local_x = lax.dynamic_slice_in_dim(inter, owner * YB, YB, 0)
    window_keys = local_x * YB + jnp.arange(YB, dtype=jnp.int32)[:, None]
    picked, source = pick(arrived, window_keys.reshape(-1), tile)
    col_len = lax.dynamic_slice_in_dim(lengths, me * YB, YB, 0)
    row_len = lengths[:x_count]
    key = (inter * YB).reshape(-1)

    outgoing = pack(posteriors, slot_target, devices)
    outgoing, picked, source, col_len, row_len, key = lax.optimization_barrier(
        (outgoing, picked, source, col_len, row_len, key)
    )
    window = lax.all_gather(picked, AXES, axis=0, tiled=False)
    incoming = lax.all_to_all(outgoing, AXES, split_axis=0, concat_axis=0, tiled=True)
    window = window.reshape(pieces, x_count * INTER, tile, side)
    return transform(incoming, window, source, key, row_len, col_len)


def solution(mesh):
    return jax.shard_map(
        shards,
        mesh=mesh,
        in_specs=(P(AXES, None, None), P(AXES), P(AXES), P(), P()),
        out_specs=P(None, AXES, None, None),
        check_vma=False,
    )
```

```python
import functools

import jax
import jax.numpy as jnp
from jax import lax
from jax.experimental import pallas as pl
from jax.experimental.pallas import tpu as pltpu
from jax.sharding import PartitionSpec as P

NZ = 16
INTER = 4
YB = 4
STORES = 4
AXES = ("row", "col")
VMEM_LIMIT = 56 * 1024 * 1024
SMALL_VMEM = 8 * 1024 * 1024


def pack_kernel(slot_target_ref, blocks_ref, out_ref, held_ref, load_sems, store_sem):
    chunks = load_sems.shape[0]
    slots = held_ref.shape[0]
    chunk = slots // chunks

    def load(c):
        part = pl.ds(c * chunk, chunk)
        return pltpu.make_async_copy(blocks_ref.at[part], held_ref.at[part], load_sems.at[c])

    for c in range(chunks):
        load(c).start()
    for c in range(chunks):
        load(c).wait()
        for s in range(c * chunk, (c + 1) * chunk):
            pltpu.make_async_copy(
                held_ref.at[s], out_ref.at[slot_target_ref[s]], store_sem
            ).start()
    pltpu.make_async_copy(held_ref, out_ref.at[pl.ds(0, slots)], store_sem).wait()


def pack(posteriors, slot_target, devices):
    slots, side, _ = posteriors.shape
    chunks = 8
    return pl.pallas_call(
        pack_kernel,
        out_shape=jax.ShapeDtypeStruct((devices, side, side), posteriors.dtype),
        in_specs=[
            pl.BlockSpec(memory_space=pltpu.SMEM),
            pl.BlockSpec(memory_space=pl.ANY),
        ],
        out_specs=pl.BlockSpec(memory_space=pl.ANY),
        scratch_shapes=[
            pltpu.VMEM((slots, side, side), posteriors.dtype),
            pltpu.SemaphoreType.DMA((chunks,)),
            pltpu.SemaphoreType.DMA,
        ],
        compiler_params=pltpu.CompilerParams(vmem_limit_bytes=VMEM_LIMIT),
        name="pack",
    )(slot_target, posteriors)


def pieces_kernel(owner_slot_ref, sent_key_ref, blocks_ref, out_ref, held_ref, sems):
    pieces, owners, rows, half = out_ref.shape
    side = 2 * half
    tile = side // pieces
    header = 2 * tile

    def load(o):
        return pltpu.make_async_copy(
            blocks_ref.at[owner_slot_ref[o]], held_ref.at[o], sems.at[o]
        )

    for o in range(owners):
        load(o).start()
    first = lax.broadcasted_iota(jnp.int32, (rows - header, half), 0) < (rows - header) // 2
    for o in range(owners):
        for p in range(pieces):
            keys = jnp.where(first, sent_key_ref[p * owners + o], sent_key_ref[o])
            out_ref[p, o, header:, :] = keys.astype(jnp.float32).astype(out_ref.dtype)
    for o in range(owners):
        load(o).wait()
        turned = held_ref[o].T
        for part in range(2):
            out_ref[:, o, part * tile : (part + 1) * tile, :] = turned[
                :, part * half : (part + 1) * half
            ].reshape(pieces, tile, half)


def window_pieces(posteriors, owner_slot, sent_key, pieces):
    _, side, _ = posteriors.shape
    owners = owner_slot.shape[0]
    rows = 2 * side // pieces + 8
    return pl.pallas_call(
        pieces_kernel,
        out_shape=jax.ShapeDtypeStruct((pieces, owners, rows, side // 2), posteriors.dtype),
        in_specs=[pl.BlockSpec(memory_space=pltpu.SMEM)] * 2 + [pl.BlockSpec(memory_space=pl.ANY)],
        out_specs=pl.BlockSpec(memory_space=pltpu.VMEM),
        scratch_shapes=[
            pltpu.VMEM((owners, side, side), posteriors.dtype),
            pltpu.SemaphoreType.DMA((owners,)),
        ],
        compiler_params=pltpu.CompilerParams(vmem_limit_bytes=VMEM_LIMIT),
        name="pieces",
    )(owner_slot, sent_key, posteriors)


def pick_kernel(wanted_ref, arrived_ref, picked_ref, source_ref, found_ref, where_ref, sem):
    wanted, tile, side = picked_ref.shape
    devices, _, half = arrived_ref.shape
    keys = lax.broadcasted_iota(jnp.int32, (devices, half), 1)
    device = lax.broadcasted_iota(jnp.int32, (devices, half), 0)
    for part in range(2):
        got = arrived_ref[:, 2 * tile + 4 * part, :].astype(jnp.float32).astype(jnp.int32)
        found = jnp.sum(jnp.where(got == keys, device, 0), axis=0, keepdims=True)
        found_ref[pl.ds(part, 1), :] = found
    source_ref[...] = found_ref[pl.ds(0, 1), :]
    copy = pltpu.make_async_copy(found_ref, where_ref, sem)
    copy.start()
    copy.wait()
    for q in range(wanted):
        sender = where_ref[1, wanted_ref[q]]
        picked_ref[q, :, :half] = arrived_ref[sender, :tile, :]
        picked_ref[q, :, half:] = arrived_ref[sender, tile : 2 * tile, :]


def pick(arrived, wanted, tile):
    half = arrived.shape[2]
    count = wanted.shape[0]
    return pl.pallas_call(
        pick_kernel,
        out_shape=(
            jax.ShapeDtypeStruct((count, tile, 2 * half), arrived.dtype),
            jax.ShapeDtypeStruct((1, half), jnp.int32),
        ),
        in_specs=[
            pl.BlockSpec(memory_space=pltpu.SMEM),
            pl.BlockSpec(memory_space=pltpu.VMEM),
        ],
        out_specs=(pl.BlockSpec(memory_space=pltpu.VMEM), pl.BlockSpec(memory_space=pltpu.VMEM)),
        scratch_shapes=[
            pltpu.VMEM((2, half), jnp.int32),
            pltpu.SMEM((2, half), jnp.int32),
            pltpu.SemaphoreType.DMA,
        ],
        compiler_params=pltpu.CompilerParams(vmem_limit_bytes=SMALL_VMEM),
        name="pick",
    )(wanted, arrived)


def transform_kernel(
    source_ref,
    key_ref,
    row_len_ref,
    col_len_ref,
    window_ref,
    incoming_ref,
    out_ref,
    slab_ref,
    left_ref,
    held_ref,
    slab_sems,
    left_sems,
    out_sems,
):
    keys, side, _ = slab_ref.shape
    count, pieces, _, tile, _ = left_ref.shape
    depth = held_ref.shape[0]

    def fetch_left(g):
        return pltpu.make_async_copy(
            window_ref.at[:, pl.ds(g * INTER, INTER)], left_ref.at[g], left_sems.at[g]
        )

    def store(g, slot):
        return pltpu.make_async_copy(held_ref.at[slot], out_ref.at[g], out_sems.at[slot])

    def fetch(k, sem):
        pltpu.make_async_copy(incoming_ref.at[source_ref[0, k]], slab_ref.at[k], sem).start()

    def wait_blocks(amount, sem):
        part = pl.ds(0, amount)
        pltpu.make_async_copy(incoming_ref.at[part], slab_ref.at[part], sem).wait()

    def fetch_other(anchor, carry):
        used = [key_ref[k] == anchor * YB for k in range(INTER)]

        @pl.when(~functools.reduce(jnp.logical_or, used))
        def _():
            for y in range(YB):
                fetch(anchor * YB + y, slab_sems.at[1])

        return carry

    def start_left(g, carry):
        fetch_left(g).start()
        return carry

    fetch_left(0).start()
    for k in range(INTER):
        for y in range(YB):
            fetch(key_ref[k] + y, slab_sems.at[0])
    lax.fori_loop(0, keys // YB, fetch_other, 0)
    lax.fori_loop(1, count, start_left, 0)
    wait_blocks(INTER * YB, slab_sems.at[0])

    def one_row(g, carry):
        slot = lax.rem(g, depth)
        row_len = row_len_ref[g]
        fetch_left(g).wait()

        @pl.when(g == 1)
        def _():
            wait_blocks(keys - INTER * YB, slab_sems.at[1])

        @pl.when(g >= depth)
        def _():
            store(g - depth, slot).wait()

        def compute(height):
            lanes = lax.broadcasted_iota(jnp.int32, (height, side), 1)
            rows = lax.broadcasted_iota(jnp.int32, (height, side), 0)
            lefts = [left_ref[g, : height // tile, k].reshape(height, side) for k in range(INTER)]
            for y in range(YB):
                total = jnp.dot(
                    lefts[0], slab_ref[key_ref[g * INTER] + y], preferred_element_type=jnp.float32
                )
                for k in range(1, INTER):
                    total += jnp.dot(
                        lefts[k],
                        slab_ref[key_ref[g * INTER + k] + y],
                        preferred_element_type=jnp.float32,
                    )
                keep = (rows < row_len) & (lanes < col_len_ref[y])
                held_ref[slot, y, :height, :] = jnp.where(
                    keep, total * (1.0 / INTER), 0.0
                ).astype(held_ref.dtype)

        @pl.when(row_len > side // 2)
        def _():
            compute(side)

        @pl.when(row_len <= side // 2)
        def _():
            compute(side // 2)
            held_ref[slot, :, side // 2 :, :] = jnp.zeros((YB, side // 2, side), held_ref.dtype)

        store(g, slot).start()
        return carry

    lax.fori_loop(0, count, one_row, 0)
    for g in range(count - depth, count):
        store(g, g % depth).wait()


def transform(incoming, window, source, key, row_len, col_len):
    pieces, entries, tile, side = window.shape
    count = entries // INTER
    keys = NZ * YB
    anywhere = pl.BlockSpec(memory_space=pl.ANY)
    return pl.pallas_call(
        transform_kernel,
        out_shape=jax.ShapeDtypeStruct((row_len.shape[0], YB, side, side), incoming.dtype),
        in_specs=[pl.BlockSpec(memory_space=pltpu.SMEM)] * 4 + [anywhere] * 2,
        out_specs=anywhere,
        scratch_shapes=[
            pltpu.VMEM((keys, side, side), incoming.dtype),
            pltpu.VMEM((count, pieces, INTER, tile, side), incoming.dtype),
            pltpu.VMEM((STORES, YB, side, side), incoming.dtype),
            pltpu.SemaphoreType.DMA((2,)),
            pltpu.SemaphoreType.DMA((count,)),
            pltpu.SemaphoreType.DMA((STORES,)),
        ],
        cost_estimate=pl.CostEstimate(
            flops=2 * count * YB * INTER * side**3,
            bytes_accessed=2 * (keys + count * (YB + INTER)) * side * side,
            transcendentals=0,
        ),
        compiler_params=pltpu.CompilerParams(vmem_limit_bytes=VMEM_LIMIT),
        name="transform",
    )(source, key, row_len, col_len, window, incoming)


def shards(posteriors, pair_anchor, pair_column, inter, lengths):
    devices = lax.axis_size(AXES)
    pieces = lax.axis_size("row")
    owners = lax.axis_size("col")
    me = lax.axis_index(AXES)
    owner = lax.axis_index("col")
    slots, side, _ = posteriors.shape
    x_count = inter.shape[0]
    tile = side // pieces

    slot_target = pair_column // YB
    slot_key = pair_anchor * YB + pair_column % YB
    aims = slot_target[None, :] == jnp.arange(devices, dtype=jnp.int32)[:, None]
    sent_key = slots + jnp.sum(jnp.where(aims, slot_key[None, :] - slots, 0), axis=1)
    slot_ids = jnp.arange(slots, dtype=jnp.int32)
    owner_slot = jnp.sum(jnp.where(aims[:owners], slot_ids[None, :], 0), axis=1)

    cut = window_pieces(posteriors, owner_slot, sent_key, pieces)
    arrived = lax.all_to_all(
        cut.reshape(devices, 2 * tile + 8, side // 2), AXES, split_axis=0, concat_axis=0, tiled=True
    )

    local_x = lax.dynamic_slice_in_dim(inter, owner * YB, YB, 0)
    window_keys = local_x * YB + jnp.arange(YB, dtype=jnp.int32)[:, None]
    picked, source = pick(arrived, window_keys.reshape(-1), tile)
    col_len = lax.dynamic_slice_in_dim(lengths, me * YB, YB, 0)
    row_len = lengths[:x_count]
    key = (inter * YB).reshape(-1)

    outgoing = pack(posteriors, slot_target, devices)
    outgoing, picked, source, col_len, row_len, key = lax.optimization_barrier(
        (outgoing, picked, source, col_len, row_len, key)
    )
    window = lax.all_gather(picked, AXES, axis=0, tiled=False)
    incoming = lax.all_to_all(outgoing, AXES, split_axis=0, concat_axis=0, tiled=True)
    window = window.reshape(pieces, x_count * INTER, tile, side)
    return transform(incoming, window, source, key, row_len, col_len)


def solution(mesh):
    return jax.shard_map(
        shards,
        mesh=mesh,
        in_specs=(P(AXES, None, None), P(AXES), P(AXES), P(), P()),
        out_specs=P(None, AXES, None, None),
        check_vma=False,
    )
```

```python
import functools

import jax
import jax.numpy as jnp
from jax import lax
from jax.experimental import pallas as pl
from jax.experimental.pallas import tpu as pltpu
from jax.sharding import PartitionSpec as P

NZ = 16
INTER = 4
YB = 4
STORES = 4
AXES = ("row", "col")
VMEM_LIMIT = 56 * 1024 * 1024
SMALL_VMEM = 8 * 1024 * 1024


def pack_kernel(column_ref, blocks_ref, out_ref, held_ref, load_sems, store_sem):
    chunks = load_sems.shape[0]
    slots = held_ref.shape[0]
    chunk = slots // chunks

    def load(c):
        part = pl.ds(c * chunk, chunk)
        return pltpu.make_async_copy(blocks_ref.at[part], held_ref.at[part], load_sems.at[c])

    for c in range(chunks):
        load(c).start()
    for c in range(chunks):
        load(c).wait()
        for s in range(c * chunk, (c + 1) * chunk):
            pltpu.make_async_copy(
                held_ref.at[s], out_ref.at[lax.div(column_ref[s], YB)], store_sem
            ).start()
    pltpu.make_async_copy(held_ref, out_ref.at[pl.ds(0, slots)], store_sem).wait()


def pack(posteriors, pair_column, devices):
    slots, side, _ = posteriors.shape
    chunks = 8
    return pl.pallas_call(
        pack_kernel,
        out_shape=jax.ShapeDtypeStruct((devices, side, side), posteriors.dtype),
        in_specs=[
            pl.BlockSpec(memory_space=pltpu.SMEM),
            pl.BlockSpec(memory_space=pl.ANY),
        ],
        out_specs=pl.BlockSpec(memory_space=pl.ANY),
        scratch_shapes=[
            pltpu.VMEM((slots, side, side), posteriors.dtype),
            pltpu.SemaphoreType.DMA((chunks,)),
            pltpu.SemaphoreType.DMA,
        ],
        compiler_params=pltpu.CompilerParams(vmem_limit_bytes=VMEM_LIMIT),
        name="pack",
    )(pair_column, posteriors)


def pieces_kernel(
    anchor_ref, column_ref, blocks_ref, out_ref, slot_ref, sent_key_ref, held_ref, sems
):
    pieces, owners, rows, half = out_ref.shape
    side = 2 * half
    tile = side // pieces
    header = 2 * tile

    def load(o):
        return pltpu.make_async_copy(
            blocks_ref.at[slot_ref[o]], held_ref.at[o], sems.at[o]
        )

    slots = anchor_ref.shape[0]

    def clear(d, carry):
        slot_ref[d] = 0
        sent_key_ref[d] = slots
        return carry

    def note(s, carry):
        target = lax.div(column_ref[s], YB)
        slot_ref[target] = s
        sent_key_ref[target] = anchor_ref[s] * YB + lax.rem(column_ref[s], YB)
        return carry

    lax.fori_loop(0, pieces * owners, clear, 0, unroll=8)
    lax.fori_loop(0, slots, note, 0, unroll=8)
    for o in range(owners):
        load(o).start()
    first = lax.broadcasted_iota(jnp.int32, (rows - header, half), 0) < (rows - header) // 2
    for o in range(owners):
        for p in range(pieces):
            keys = jnp.where(first, sent_key_ref[p * owners + o], sent_key_ref[o])
            out_ref[p, o, header:, :] = keys.astype(jnp.float32).astype(out_ref.dtype)
    for o in range(owners):
        load(o).wait()
        turned = held_ref[o].T
        for part in range(2):
            out_ref[:, o, part * tile : (part + 1) * tile, :] = turned[
                :, part * half : (part + 1) * half
            ].reshape(pieces, tile, half)


def window_pieces(posteriors, pair_anchor, pair_column, pieces, owners):
    _, side, _ = posteriors.shape
    rows = 2 * side // pieces + 8
    return pl.pallas_call(
        pieces_kernel,
        out_shape=jax.ShapeDtypeStruct((pieces, owners, rows, side // 2), posteriors.dtype),
        in_specs=[pl.BlockSpec(memory_space=pltpu.SMEM)] * 2 + [pl.BlockSpec(memory_space=pl.ANY)],
        out_specs=pl.BlockSpec(memory_space=pltpu.VMEM),
        scratch_shapes=[
            pltpu.SMEM((pieces * owners,), jnp.int32),
            pltpu.SMEM((pieces * owners,), jnp.int32),
            pltpu.VMEM((owners, side, side), posteriors.dtype),
            pltpu.SemaphoreType.DMA((owners,)),
        ],
        compiler_params=pltpu.CompilerParams(vmem_limit_bytes=VMEM_LIMIT),
        name="pieces",
    )(pair_anchor, pair_column, posteriors)


def pick_kernel(wanted_ref, arrived_ref, picked_ref, source_ref, found_ref, where_ref, sem):
    wanted, tile, side = picked_ref.shape
    devices, _, half = arrived_ref.shape
    keys = lax.broadcasted_iota(jnp.int32, (devices, half), 1)
    device = lax.broadcasted_iota(jnp.int32, (devices, half), 0)
    for part in range(2):
        got = arrived_ref[:, 2 * tile + 4 * part, :].astype(jnp.float32).astype(jnp.int32)
        found = jnp.sum(jnp.where(got == keys, device, 0), axis=0, keepdims=True)
        found_ref[pl.ds(part, 1), :] = found
    source_ref[...] = found_ref[pl.ds(0, 1), :]
    copy = pltpu.make_async_copy(found_ref, where_ref, sem)
    copy.start()
    copy.wait()
    for q in range(wanted):
        sender = where_ref[1, wanted_ref[q]]
        picked_ref[q, :, :half] = arrived_ref[sender, :tile, :]
        picked_ref[q, :, half:] = arrived_ref[sender, tile : 2 * tile, :]


def pick(arrived, wanted, tile):
    half = arrived.shape[2]
    count = wanted.shape[0]
    return pl.pallas_call(
        pick_kernel,
        out_shape=(
            jax.ShapeDtypeStruct((count, tile, 2 * half), arrived.dtype),
            jax.ShapeDtypeStruct((1, half), jnp.int32),
        ),
        in_specs=[
            pl.BlockSpec(memory_space=pltpu.SMEM),
            pl.BlockSpec(memory_space=pltpu.VMEM),
        ],
        out_specs=(pl.BlockSpec(memory_space=pltpu.VMEM), pl.BlockSpec(memory_space=pltpu.VMEM)),
        scratch_shapes=[
            pltpu.VMEM((2, half), jnp.int32),
            pltpu.SMEM((2, half), jnp.int32),
            pltpu.SemaphoreType.DMA,
        ],
        compiler_params=pltpu.CompilerParams(vmem_limit_bytes=SMALL_VMEM),
        name="pick",
    )(wanted, arrived)


def transform_kernel(
    source_ref,
    key_ref,
    row_len_ref,
    col_len_ref,
    window_ref,
    incoming_ref,
    out_ref,
    slab_ref,
    left_ref,
    held_ref,
    slab_sems,
    left_sems,
    out_sems,
):
    keys, side, _ = slab_ref.shape
    count, pieces, _, tile, _ = left_ref.shape
    depth = held_ref.shape[0]

    def fetch_left(g):
        return pltpu.make_async_copy(
            window_ref.at[:, pl.ds(g * INTER, INTER)], left_ref.at[g], left_sems.at[g]
        )

    def store(g, slot):
        return pltpu.make_async_copy(held_ref.at[slot], out_ref.at[g], out_sems.at[slot])

    def fetch(k, sem):
        pltpu.make_async_copy(incoming_ref.at[source_ref[0, k]], slab_ref.at[k], sem).start()

    def wait_blocks(amount, sem):
        part = pl.ds(0, amount)
        pltpu.make_async_copy(incoming_ref.at[part], slab_ref.at[part], sem).wait()

    def fetch_other(anchor, carry):
        used = [key_ref[k] == anchor * YB for k in range(INTER)]

        @pl.when(~functools.reduce(jnp.logical_or, used))
        def _():
            for y in range(YB):
                fetch(anchor * YB + y, slab_sems.at[1])

        return carry

    def start_left(g, carry):
        fetch_left(g).start()
        return carry

    fetch_left(0).start()
    for k in range(INTER):
        for y in range(YB):
            fetch(key_ref[k] + y, slab_sems.at[0])
    lax.fori_loop(0, keys // YB, fetch_other, 0)
    lax.fori_loop(1, count, start_left, 0)
    wait_blocks(INTER * YB, slab_sems.at[0])

    def one_row(g, carry):
        slot = lax.rem(g, depth)
        row_len = row_len_ref[g]
        fetch_left(g).wait()

        @pl.when(g == 1)
        def _():
            wait_blocks(keys - INTER * YB, slab_sems.at[1])

        @pl.when(g >= depth)
        def _():
            store(g - depth, slot).wait()

        def compute(height):
            lanes = lax.broadcasted_iota(jnp.int32, (height, side), 1)
            rows = lax.broadcasted_iota(jnp.int32, (height, side), 0)
            lefts = [left_ref[g, : height // tile, k].reshape(height, side) for k in range(INTER)]
            for y in range(YB):
                total = jnp.dot(
                    lefts[0], slab_ref[key_ref[g * INTER] + y], preferred_element_type=jnp.float32
                )
                for k in range(1, INTER):
                    total += jnp.dot(
                        lefts[k],
                        slab_ref[key_ref[g * INTER + k] + y],
                        preferred_element_type=jnp.float32,
                    )
                keep = (rows < row_len) & (lanes < col_len_ref[y])
                held_ref[slot, y, :height, :] = jnp.where(
                    keep, total * (1.0 / INTER), 0.0
                ).astype(held_ref.dtype)

        @pl.when(row_len > side // 2)
        def _():
            compute(side)

        @pl.when(row_len <= side // 2)
        def _():
            compute(side // 2)
            held_ref[slot, :, side // 2 :, :] = jnp.zeros((YB, side // 2, side), held_ref.dtype)

        store(g, slot).start()
        return carry

    lax.fori_loop(0, count, one_row, 0)
    for g in range(count - depth, count):
        store(g, g % depth).wait()


def transform(incoming, window, source, key, row_len, col_len):
    pieces, entries, tile, side = window.shape
    count = entries // INTER
    keys = NZ * YB
    anywhere = pl.BlockSpec(memory_space=pl.ANY)
    return pl.pallas_call(
        transform_kernel,
        out_shape=jax.ShapeDtypeStruct((row_len.shape[0], YB, side, side), incoming.dtype),
        in_specs=[pl.BlockSpec(memory_space=pltpu.SMEM)] * 4 + [anywhere] * 2,
        out_specs=anywhere,
        scratch_shapes=[
            pltpu.VMEM((keys, side, side), incoming.dtype),
            pltpu.VMEM((count, pieces, INTER, tile, side), incoming.dtype),
            pltpu.VMEM((STORES, YB, side, side), incoming.dtype),
            pltpu.SemaphoreType.DMA((2,)),
            pltpu.SemaphoreType.DMA((count,)),
            pltpu.SemaphoreType.DMA((STORES,)),
        ],
        cost_estimate=pl.CostEstimate(
            flops=2 * count * YB * INTER * side**3,
            bytes_accessed=2 * (keys + count * (YB + INTER)) * side * side,
            transcendentals=0,
        ),
        compiler_params=pltpu.CompilerParams(vmem_limit_bytes=VMEM_LIMIT),
        name="transform",
    )(source, key, row_len, col_len, window, incoming)


def shards(posteriors, pair_anchor, pair_column, inter, lengths):
    devices = lax.axis_size(AXES)
    pieces = lax.axis_size("row")
    owners = lax.axis_size("col")
    me = lax.axis_index(AXES)
    owner = lax.axis_index("col")
    side = posteriors.shape[1]
    x_count = inter.shape[0]
    tile = side // pieces

    cut = window_pieces(posteriors, pair_anchor, pair_column, pieces, owners)
    arrived = lax.all_to_all(
        cut.reshape(devices, 2 * tile + 8, side // 2), AXES, split_axis=0, concat_axis=0, tiled=True
    )

    local_x = lax.dynamic_slice_in_dim(inter, owner * YB, YB, 0)
    window_keys = local_x * YB + jnp.arange(YB, dtype=jnp.int32)[:, None]
    picked, source = pick(arrived, window_keys.reshape(-1), tile)
    col_len = lax.dynamic_slice_in_dim(lengths, me * YB, YB, 0)
    row_len = lengths[:x_count]
    key = (inter * YB).reshape(-1)

    outgoing = pack(posteriors, pair_column, devices)
    outgoing, picked, source, col_len, row_len, key = lax.optimization_barrier(
        (outgoing, picked, source, col_len, row_len, key)
    )
    window = lax.all_gather(picked, AXES, axis=0, tiled=False)
    incoming = lax.all_to_all(outgoing, AXES, split_axis=0, concat_axis=0, tiled=True)
    window = window.reshape(pieces, x_count * INTER, tile, side)
    return transform(incoming, window, source, key, row_len, col_len)


def solution(mesh):
    return jax.shard_map(
        shards,
        mesh=mesh,
        in_specs=(P(AXES, None, None), P(AXES), P(AXES), P(), P()),
        out_specs=P(None, AXES, None, None),
        check_vma=False,
    )
```
